256 devices in a mesh: section: 16 (over x, z_hi), dp: 16 (over z_lo, y, core).
Axes of the slice: x: 4, y: 4, z: 8 (z_hi: 4, z_lo: 2; z = z_hi * 2 + z_lo), core: 2. Of those that a mesh axis runs over, the one named last changes fastest.
Arguments:
- section_inputs: bfloat16 [16, 768, 1152], P('section'), may hold values from -6 to 6
- mirror_held: bfloat16 [16, 768, 1152], P('section'), may hold values from -6 to 6
- section_cotangents: bfloat16 [16, 768, 1152], P('section'), may hold values from -6 to 6
- next_batch: bfloat16 [768, 1152], replicated, may hold values from -6 to 6
- loss_cotangent: bfloat16 [768, 1152], replicated, may hold values from -6 to 6
- join_weights: bfloat16 [16, 1152, 1152], P('section'), may hold values from -0.125 to 0.125
Outputs:
- section_outputs: bfloat16 [256, 2, 768, 1152], P(('dp', 'section')), parts along dimension 0
- section_gradients: bfloat16 [256, 2, 768, 1152], P(('dp', 'section')), parts along dimension 0
- mirror_arrivals: bfloat16 [256, 768, 1152], P(('dp', 'section')), parts along dimension 0
The draws below stay inside these ranges and needn't reach their ends.
There are 16 independent parts, one for each index of `dp`. The reference program is written for one: setup_inputs(seed, part) draws one part's arguments, and reference() takes and returns one part's arrays. A program takes and returns all parts, laid end to end along the dimension named above; an argument that names none is the same for every part. Nothing has to cross between parts.
All inputs are finite; a program needn't handle non-finite values.
Results may differ from the reference program's by a relative error of at most 0.001.
Values may be sent and summed in bfloat16 or wider, within the bound.
No kernel may reach another device: no remote copies, remote signals or barrier semaphores. Data moves between devices by JAX's collectives and lax.ppermute only.
A program may use at most 128 MiB of HBM per device.

```python
import jax
import jax.numpy as jnp

D = 1152
ROWS = 768
SECTIONS = 16


def steps_of(rng, extent, shards, smallest, largest):
    def one(position, shards_of):
        steps = jax.random.uniform(jax.random.fold_in(jax.random.fold_in(rng, 6), position), (shards_of,), jnp.float32, smallest / len(shards), largest / len(shards))
        return jnp.repeat(jnp.exp(steps), extent[position] // shards_of).reshape((-1,) + (1,) * (len(extent) - position - 1))

    loudness = one(*shards[0])
    for cut in shards[1:]:
        loudness = loudness * one(*cut)
    return loudness


def gaussian(rng, dims, deviation, most, cuts=(), kind=jnp.bfloat16):
    drawn = deviation * jax.random.normal(rng, dims, jnp.float32)
    if cuts:
        drawn = drawn * steps_of(rng, dims, cuts, -0.22, 0.18)
    return jnp.clip(drawn, -most, most).astype(kind)


def setup_inputs(seed: int = 0, part: int = 0) -> dict:
    key_of = jax.random.split(jax.random.key(seed), 7)
    section_inputs = gaussian(key_of[0], (SECTIONS, ROWS, D), 1.0, 6.0, ((0, 16),))
    mirror_held = gaussian(key_of[1], (SECTIONS, ROWS, D), 1.0, 6.0, ((0, 16),))
    section_cotangents = gaussian(key_of[2], (SECTIONS, ROWS, D), 1.0, 6.0, ((0, 16),))
    next_batch = gaussian(key_of[3], (ROWS, D), 1.0, 6.0)
    loss_cotangent = gaussian(key_of[4], (ROWS, D), 1.0, 6.0)
    join_weights = gaussian(key_of[5], (SECTIONS, D, D), (2 * D) ** -0.5, 0.125, ((0, 16),))
    return dict(section_inputs=section_inputs, mirror_held=mirror_held, section_cotangents=section_cotangents, next_batch=next_batch, loss_cotangent=loss_cotangent, join_weights=join_weights)


def slot_tables(count):
    slots = jnp.arange(count, dtype=jnp.int32)
    even = slots % 2 == 0
    partner = slots + 1 - 2 * (slots % 2)
    before = jnp.where(even, slots - 2, jnp.where(slots == count - 1, count - 2, slots + 2))
    after = jnp.where(even, jnp.where(slots == count - 2, count - 1, slots + 2), slots - 2)
    before = jnp.clip(before, 0, count - 1).astype(jnp.int32)
    after = jnp.clip(after, 0, count - 1).astype(jnp.int32)
    return slots, even[:, None, None], partner.astype(jnp.int32), before, after


def forward_tick(arriving, pending, join_weights, even, partner):
    product = jnp.einsum("srd,sde->sre", arriving.astype(jnp.float32), join_weights.astype(jnp.float32))
    projected = product.astype(jnp.bfloat16)
    joined = (product + pending.astype(jnp.float32)).astype(jnp.bfloat16)
    leaving = jnp.where(even, arriving, joined)
    return leaving, projected[partner]


def backward_tick(cotangent, returned, join_weights, even, partner):
    operand = jnp.where(even, returned, cotangent)
    product = jnp.einsum("sre,sde->srd", operand.astype(jnp.float32), join_weights.astype(jnp.float32))
    grad = jnp.where(even, cotangent.astype(jnp.float32) + product, product).astype(jnp.bfloat16)
    return grad, cotangent[partner]


def reference(section_inputs, mirror_held, section_cotangents, next_batch, loss_cotangent, join_weights):
    count = section_inputs.shape[0]
    slots, even, partner, before, after = slot_tables(count)
    first_out, skips_one = forward_tick(section_inputs, mirror_held, join_weights, even, partner)
    first_grad, returns_one = backward_tick(section_cotangents, mirror_held, join_weights, even, partner)
    second_in = jnp.where((slots == 0)[:, None, None], next_batch[None], first_out[before])
    second_out, skips_two = forward_tick(second_in, skips_one, join_weights, even, partner)
    second_cot = jnp.where((slots == 1)[:, None, None], loss_cotangent[None], first_grad[after])
    second_grad, returns_two = backward_tick(second_cot, returns_one, join_weights, even, partner)
    section_outputs = jnp.stack([first_out, second_out], axis=1)
    section_gradients = jnp.stack([first_grad, second_grad], axis=1)
    mirror_arrivals = jnp.where(even, returns_two, skips_two)
    return section_outputs, section_gradients, mirror_arrivals
```

```python
import jax
import jax.numpy as jnp
from jax import lax
from jax.sharding import PartitionSpec as P


def relay_pairs(count):
    order = list(range(0, count, 2)) + list(range(count - 1, 0, -2))
    return list(zip(order[:-1], order[1:]))


def local(
    section_inputs, mirror_held, section_cotangents, next_batch, loss_cotangent, join_weights
):
    count = lax.axis_size("section")
    replicas = lax.axis_size("dp")
    position = lax.axis_index("section")
    is_early = position % 2 == 0
    weights = join_weights[0]
    rows = next_batch.shape[0] // replicas
    start = lax.axis_index("dp") * rows

    ahead = relay_pairs(count)
    back = [(b, a) for a, b in ahead]
    mirror = [(i, i ^ 1) for i in range(count)]

    def times(left):
        return jnp.dot(left, weights, preferred_element_type=jnp.float32)

    def times_t(left):
        return lax.dot_general(
            left, weights, (((1,), (1,)), ((), ())), preferred_element_type=jnp.float32
        )

    def forward(arriving, pending):
        product = times(arriving)
        joined = (product + pending.astype(jnp.float32)).astype(jnp.bfloat16)
        return jnp.where(is_early, arriving, joined), product.astype(jnp.bfloat16)

    def backward(cotangent, returned):
        product = times_t(jnp.where(is_early, returned, cotangent))
        return jnp.where(is_early, cotangent.astype(jnp.float32) + product, product).astype(
            jnp.bfloat16
        )

    def part(whole):
        return lax.dynamic_slice_in_dim(whole, start, rows, 0)

    a, held, cot = section_inputs[0], mirror_held[0], section_cotangents[0]
    a_part, held_part, cot_part = part(a), part(held), part(cot)
    out_part, skip_part = forward(a_part, held_part)
    grad_part = backward(cot_part, held_part)
    came_out = lax.ppermute(out_part, "section", ahead)
    came_grad = lax.ppermute(grad_part, "section", back)
    came_mirror = lax.ppermute(jnp.where(is_early, skip_part, cot_part), "section", mirror)
    second_in = jnp.where(position == 0, part(next_batch), came_out)
    second_cot = jnp.where(position == 1, part(loss_cotangent), came_grad)
    second_out, second_skip = forward(second_in, came_mirror)
    second_grad = backward(second_cot, came_mirror)
    arrived = lax.ppermute(jnp.where(is_early, second_skip, second_cot), "section", mirror)
    parts = jnp.stack([second_out, second_grad, arrived], axis=0)
    whole = lax.all_gather(parts, "dp", axis=1, tiled=True)

    first_out, _ = forward(a, held)
    first_grad = backward(cot, held)
    section_outputs = jnp.stack([first_out, whole[0]], axis=0)[None]
    section_gradients = jnp.stack([first_grad, whole[1]], axis=0)[None]
    return (section_outputs, section_gradients, whole[2][None])


def solution(mesh):
    in_specs = (
        P("section", None, None),
        P("section", None, None),
        P("section", None, None),
        P(),
        P(),
        P("section", None, None),
    )
    out_specs = (
        P(("dp", "section"), None, None, None),
        P(("dp", "section"), None, None, None),
        P(("dp", "section"), None, None),
    )
    return jax.shard_map(local, mesh=mesh, in_specs=in_specs, out_specs=out_specs, check_vma=False)
```

```python
import functools

import jax
import jax.numpy as jnp
from jax import lax
from jax.experimental import pallas as pl
from jax.experimental.pallas import tpu as pltpu
from jax.sharding import PartitionSpec as P

AXES = ("section", "dp")
BF16 = jnp.bfloat16
F32 = jnp.float32
CORE, Y_NEAR, Y_FAR, Z = 1, 2, 6, 8


def next_slot(count):
    order = list(range(0, count, 2)) + list(range(count - 1, 0, -2))
    return dict(zip(order[:-1], order[1:]))


def times(left, weights):
    return jnp.dot(left, weights, preferred_element_type=F32)


def times_t(left, weights):
    return lax.dot_general(left, weights, (((1,), (1,)), ((), ())), preferred_element_type=F32)


def first_kernel(early_ref, a_ref, h_ref, g_ref, w_ref, out_ref, grad_ref):
    early = early_ref[0] == 1

    @pl.when(early)
    def _():
        out_ref[0, 0] = a_ref[0]
        product = times_t(h_ref[0], w_ref[0])
        grad_ref[0, 0] = (g_ref[0].astype(F32) + product).astype(BF16)

    @pl.when(jnp.logical_not(early))
    def _():
        product = times(a_ref[0], w_ref[0])
        out_ref[0, 0] = (product + h_ref[0].astype(F32)).astype(BF16)
        grad_ref[0, 0] = times_t(g_ref[0], w_ref[0]).astype(BF16)


def first_tick(early, a, held, cot, weights):
    _, height, width = a.shape
    block = height // 4
    rows = pl.BlockSpec((1, block, width), lambda i: (0, i, 0))
    wide = pl.BlockSpec((1, 1, block, width), lambda i: (0, 0, i, 0))
    both = jax.ShapeDtypeStruct((1, 2, height, width), BF16)
    return pl.pallas_call(
        first_kernel,
        grid=(4,),
        in_specs=[
            pl.BlockSpec(memory_space=pltpu.SMEM),
            rows,
            rows,
            rows,
            pl.BlockSpec((1, width, width), lambda i: (0, 0, 0)),
        ],
        out_specs=[wide, wide],
        out_shape=[both, both],
        cost_estimate=pl.CostEstimate(
            flops=4 * height * width * width, bytes_accessed=14 * height * width, transcendentals=0
        ),
        name="first_tick",
    )(early, a, held, cot, weights)


def place_kernel(masks, rows, replica_ref, *refs):
    pieces = [refs[4 * k : 4 * k + 4] for k in range(3)]
    out_ref, grad_ref, arrived_ref, sem = refs[14:]
    replica = replica_ref[0]
    copies = []
    for target, four, owners in zip((out_ref.at[0, 1], grad_ref.at[0, 1], arrived_ref.at[0]), pieces, masks):
        for piece, owned in zip(four, owners):
            for k, mask in enumerate(owned):
                at = pl.multiple_of((replica ^ mask) * rows, rows)
                copies.append(
                    pltpu.make_async_copy(
                        piece.at[pl.ds(k * rows, rows)],
                        target.at[pl.ds(at, rows)],
                        sem.at[len(copies)],
                    )
                )
    for copy in copies:
        copy.start()
    for copy in copies:
        copy.wait()


def place(replica, pieces, masks, outs, grads, rows):
    anywhere = pl.BlockSpec(memory_space=pl.ANY)
    flat = [piece for four in pieces for piece in four]
    return pl.pallas_call(
        functools.partial(place_kernel, masks, rows),
        in_specs=[pl.BlockSpec(memory_space=pltpu.SMEM)]
        + [pl.BlockSpec(memory_space=pltpu.VMEM)] * 12
        + [anywhere] * 2,
        out_specs=[anywhere] * 3,
        out_shape=[
            jax.ShapeDtypeStruct(outs.shape, BF16),
            jax.ShapeDtypeStruct(grads.shape, BF16),
            jax.ShapeDtypeStruct((1,) + outs.shape[2:], BF16),
        ],
        scratch_shapes=[pltpu.SemaphoreType.DMA((48,))],
        input_output_aliases={13: 0, 14: 1},
        name="place",
    )(replica, *flat, outs, grads)


def local(
    section_inputs, mirror_held, section_cotangents, next_batch, loss_cotangent, join_weights
):
    count = lax.axis_size("section")
    replicas = lax.axis_size("dp")
    position = lax.axis_index("section")
    replica = lax.axis_index("dp")
    is_early = position % 2 == 0
    weights = join_weights[0]
    rows = next_batch.shape[0] // replicas

    def pairs(slots, flip):
        return [
            (s * replicas + d, t * replicas + (d ^ flip))
            for s, t in slots
            for d in range(replicas)
        ]

    def send(value, *moves):
        return lax.ppermute(value, AXES, sum((pairs(slots, flip) for slots, flip in moves), []))

    def part(whole, of):
        return lax.dynamic_slice_in_dim(whole, of * rows, rows, 0)

    after = next_slot(count)
    early = range(0, count, 2)
    late = range(1, count, 2)
    a_ahead = [(s, after[s]) for s in early]
    out_ahead = [(s, after[s]) for s in late if s in after]
    grad_back = [(t, s) for s, t in after.items()]
    to_late = [(s, s + 1) for s in early]
    to_early = [(s, s - 1) for s in late]
    grad_across = [(s, s + 1) for s in late if s + 1 < count]

    sent = replica ^ Z
    a, held, cot = section_inputs[0], mirror_held[0], section_cotangents[0]
    a_part, held_part, cot_part = part(a, sent), part(held, sent), part(cot, sent)
    came_in = send(a_part, (a_ahead, Z))
    product = times(a_part, weights)
    came_mirror = send(
        jnp.where(is_early, product.astype(BF16), cot_part), (to_late, Z), (to_early, Z)
    )
    late_out = (product + held_part.astype(F32)).astype(BF16)
    product = times_t(jnp.where(is_early, held_part, cot_part), weights)
    grad = jnp.where(is_early, cot_part.astype(F32) + product, product).astype(BF16)
    early_back = [(s, t) for s, t in grad_back if s % 2 == 0]
    late_back = [(s, t) for s, t in grad_back if s % 2 == 1]
    came_low = send(jnp.where(is_early, grad, late_out), (early_back, Z), (out_ahead, Z))
    came_high = send(grad, (late_back, Z))

    early_in = jnp.where(position == 0, part(next_batch, replica), came_in)
    skip = times(early_in, weights).astype(BF16)
    came_across = send(jnp.where(is_early, skip, grad), (to_late, 0), (grad_across, Z))
    loss_part = part(loss_cotangent, replica)
    arrived = jnp.where(position == 0, loss_part, came_across)
    late_in = jnp.where(position == count - 1, came_in, came_low)
    late_out = (times(late_in, weights) + came_mirror.astype(F32)).astype(BF16)
    second_out = jnp.where(is_early, early_in, late_out)
    early_cot = jnp.where(position == count - 2, came_high, came_low)
    second_cot = jnp.where(is_early, early_cot, jnp.where(position == 1, loss_part, came_high))
    product = times_t(jnp.where(is_early, came_mirror, second_cot), weights)
    second_grad = jnp.where(is_early, second_cot.astype(F32) + product, product).astype(BF16)

    everyone = [(s, s) for s in range(count)]
    orders = ((Y_NEAR, Y_FAR, Z), (Y_FAR, Z, Y_NEAR), (Z, Y_NEAR, Y_FAR))
    held_rows = [second_out, second_grad, arrived]
    masks = [[0], [0], [0]]
    for step in range(2):
        came = [send(x, (everyone, order[step])) for x, order in zip(held_rows, orders)]
        held_rows = [jnp.concatenate([x, y], axis=0) for x, y in zip(held_rows, came)]
        masks = [m + [k ^ order[step] for k in m] for m, order in zip(masks, orders)]
    last = [send(x, (everyone, order[2])) for x, order in zip(held_rows, orders)]
    last_masks = [[k ^ order[2] for k in m] for m, order in zip(masks, orders)]
    pieces, owners = [], []
    for x, y, m, n in zip(held_rows, last, masks, last_masks):
        pieces.append([x, y, send(x, (everyone, CORE)), send(y, (everyone, CORE))])
        owners.append([m, n, [k ^ CORE for k in m], [k ^ CORE for k in n]])

    outs, grads = first_tick(
        jnp.reshape(is_early.astype(jnp.int32), (1,)),
        section_inputs,
        mirror_held,
        section_cotangents,
        join_weights,
    )
    return tuple(place(jnp.reshape(replica, (1,)), pieces, owners, outs, grads, rows))


def solution(mesh):
    in_specs = (
        P("section", None, None),
        P("section", None, None),
        P("section", None, None),
        P(),
        P(),
        P("section", None, None),
    )
    out_specs = (
        P(("dp", "section"), None, None, None),
        P(("dp", "section"), None, None, None),
        P(("dp", "section"), None, None),
    )
    return jax.shard_map(local, mesh=mesh, in_specs=in_specs, out_specs=out_specs, check_vma=False)
```

```python
import functools

import jax
import jax.numpy as jnp
from jax import lax
from jax.experimental import pallas as pl
from jax.experimental.pallas import tpu as pltpu
from jax.sharding import PartitionSpec as P

AXES = ("section", "dp")
BF16 = jnp.bfloat16
F32 = jnp.float32
CORE, Y_NEAR, Y_FAR, Z = 1, 2, 6, 8


def next_slot(count):
    order = list(range(0, count, 2)) + list(range(count - 1, 0, -2))
    return dict(zip(order[:-1], order[1:]))


def times(left, weights):
    return jnp.dot(left, weights, preferred_element_type=F32)


def times_t(left, weights):
    return lax.dot_general(left, weights, (((1,), (1,)), ((), ())), preferred_element_type=F32)


def first_kernel(early_ref, a_ref, h_ref, g_ref, w_ref, out_ref, grad_ref):
    early = early_ref[0] == 1

    @pl.when(early)
    def _():
        out_ref[0, 0] = a_ref[0]
        product = times_t(h_ref[0], w_ref[0])
        grad_ref[0, 0] = (g_ref[0].astype(F32) + product).astype(BF16)

    @pl.when(jnp.logical_not(early))
    def _():
        product = times(a_ref[0], w_ref[0])
        out_ref[0, 0] = (product + h_ref[0].astype(F32)).astype(BF16)
        grad_ref[0, 0] = times_t(g_ref[0], w_ref[0]).astype(BF16)


def first_tick(early, a, held, cot, weights):
    _, height, width = a.shape
    block = height // 4
    rows = pl.BlockSpec((1, block, width), lambda i: (0, i, 0))
    wide = pl.BlockSpec((1, 1, block, width), lambda i: (0, 0, i, 0))
    both = jax.ShapeDtypeStruct((1, 2, height, width), BF16)
    return pl.pallas_call(
        first_kernel,
        grid=(4,),
        in_specs=[
            pl.BlockSpec(memory_space=pltpu.SMEM),
            rows,
            rows,
            rows,
            pl.BlockSpec((1, width, width), lambda i: (0, 0, 0)),
        ],
        out_specs=[wide, wide],
        out_shape=[both, both],
        cost_estimate=pl.CostEstimate(
            flops=4 * height * width * width, bytes_accessed=14 * height * width, transcendentals=0
        ),
        compiler_params=pltpu.CompilerParams(vmem_limit_bytes=60 << 20),
        name="first_tick",
    )(early, a, held, cot, weights)


def place_kernel(masks, rows, replica_ref, *refs):
    count = sum(len(owners) for owners in masks)
    pieces, targets, sem = refs[:count], refs[-4:-1], refs[-1]
    replica = replica_ref[0]
    views = (targets[0].at[0, 1], targets[1].at[0, 1], targets[2].at[0])
    copies, at_piece = [], 0
    for target, owners in zip(views, masks):
        for owned in owners:
            for k, mask in enumerate(owned):
                at = pl.multiple_of((replica ^ mask) * rows, rows)
                copies.append(
                    pltpu.make_async_copy(
                        pieces[at_piece].at[pl.ds(k * rows, rows)],
                        target.at[pl.ds(at, rows)],
                        sem.at[len(copies)],
                    )
                )
            at_piece += 1
    for copy in copies:
        copy.start()
    for copy in copies:
        copy.wait()


def place(replica, pieces, masks, targets, rows):
    anywhere = pl.BlockSpec(memory_space=pl.ANY)
    flat = [piece for some in pieces for piece in some]
    width = targets[0].shape[-1]
    arrived = jax.ShapeDtypeStruct((1,) + targets[0].shape[2:], BF16)
    chunks = sum(len(owned) for owners in masks for owned in owners)
    return pl.pallas_call(
        functools.partial(place_kernel, masks, rows),
        in_specs=[pl.BlockSpec(memory_space=pltpu.SMEM)]
        + [pl.BlockSpec(memory_space=pltpu.VMEM)] * len(flat)
        + [anywhere] * len(targets),
        out_specs=[anywhere] * 3,
        out_shape=[jax.ShapeDtypeStruct(x.shape, BF16) for x in targets[:2]] + [arrived],
        scratch_shapes=[pltpu.SemaphoreType.DMA((chunks,))],
        input_output_aliases={1 + len(flat) + k: k for k in range(len(targets))},
        compiler_params=pltpu.CompilerParams(vmem_limit_bytes=8 << 20),
        cost_estimate=pl.CostEstimate(
            flops=0, bytes_accessed=4 * chunks * rows * width, transcendentals=0
        ),
        name="place",
    )(replica, *flat, *targets)


def local(
    section_inputs, mirror_held, section_cotangents, next_batch, loss_cotangent, join_weights
):
    count = lax.axis_size("section")
    replicas = lax.axis_size("dp")
    position = lax.axis_index("section")
    replica = lax.axis_index("dp")
    is_early = position % 2 == 0
    weights = join_weights[0]
    rows = next_batch.shape[0] // replicas

    def pairs(slots, flip):
        return [
            (s * replicas + d, t * replicas + (d ^ flip))
            for s, t in slots
            for d in range(replicas)
        ]

    def send(value, *moves):
        return lax.ppermute(value, AXES, sum((pairs(slots, flip) for slots, flip in moves), []))

    def part(whole, of):
        return lax.dynamic_slice_in_dim(whole, of * rows, rows, 0)

    after = next_slot(count)
    early = range(0, count, 2)
    late = range(1, count, 2)
    a_ahead = [(s, after[s]) for s in early]
    out_ahead = [(s, after[s]) for s in late if s in after]
    grad_back = [(t, s) for s, t in after.items()]
    to_late = [(s, s + 1) for s in early]
    to_early = [(s, s - 1) for s in late]
    grad_across = [(s, s + 1) for s in late if s + 1 < count]

    sent = replica ^ Z
    a, held, cot = section_inputs[0], mirror_held[0], section_cotangents[0]
    a_part, held_part, cot_part = part(a, sent), part(held, sent), part(cot, sent)
    came_in = send(a_part, (a_ahead, Z))
    product = times(a_part, weights)
    came_mirror = send(
        jnp.where(is_early, product.astype(BF16), cot_part), (to_late, Z), (to_early, Z)
    )
    late_out = (product + held_part.astype(F32)).astype(BF16)
    product = times_t(jnp.where(is_early, held_part, cot_part), weights)
    grad = jnp.where(is_early, cot_part.astype(F32) + product, product).astype(BF16)
    early_back = [(s, t) for s, t in grad_back if s % 2 == 0]
    late_back = [(s, t) for s, t in grad_back if s % 2 == 1]
    came_low = send(jnp.where(is_early, grad, late_out), (early_back, Z), (out_ahead, Z))
    came_high = send(grad, (late_back, Z))

    early_in = jnp.where(position == 0, part(next_batch, replica), came_in)
    skip = times(early_in, weights).astype(BF16)
    came_across = send(jnp.where(is_early, skip, grad), (to_late, 0), (grad_across, Z))
    loss_part = part(loss_cotangent, replica)
    arrived = jnp.where(position == 0, loss_part, came_across)
    late_in = jnp.where(position == count - 1, came_in, came_low)
    late_out = (times(late_in, weights) + came_mirror.astype(F32)).astype(BF16)
    second_out = jnp.where(is_early, early_in, late_out)
    early_cot = jnp.where(position == count - 2, came_high, came_low)
    second_cot = jnp.where(is_early, early_cot, jnp.where(position == 1, loss_part, came_high))
    product = times_t(jnp.where(is_early, came_mirror, second_cot), weights)
    second_grad = jnp.where(is_early, second_cot.astype(F32) + product, product).astype(BF16)

    everyone = [(s, s) for s in range(count)]
    orders = ((Y_NEAR, Y_FAR, Z), (Y_FAR, Z, Y_NEAR), (Z, Y_NEAR, Y_FAR))
    held_rows = [second_out, second_grad, arrived]
    masks = [[0], [0], [0]]
    for step in range(2):
        came = [send(x, (everyone, order[step])) for x, order in zip(held_rows, orders)]
        held_rows = [jnp.concatenate([x, y], axis=0) for x, y in zip(held_rows, came)]
        masks = [m + [k ^ order[step] for k in m] for m, order in zip(masks, orders)]
    last = [send(x, (everyone, order[2])) for x, order in zip(held_rows, orders)]
    last_masks = [[k ^ order[2] for k in m] for m, order in zip(masks, orders)]
    near = [send(x, (everyone, CORE)) for x in held_rows]
    operands = (section_inputs, mirror_held, section_cotangents, join_weights)
    held_rows, operands = lax.optimization_barrier((held_rows, operands))
    outs, grads = first_tick(jnp.reshape(is_early.astype(jnp.int32), (1,)), *operands)
    last, near, outs, grads = lax.optimization_barrier((last, near, outs, grads))
    far = [send(x, (everyone, CORE)) for x in last]
    here = jnp.reshape(replica, (1,))
    ready = [list(three) for three in zip(held_rows, last, near)]
    owners = [[m, n, [k ^ CORE for k in m]] for m, n in zip(masks, last_masks)]
    targets = place(here, ready, owners, (outs, grads), rows)
    owners = [[[k ^ CORE for k in n]] for n in last_masks]
    return tuple(place(here, [[x] for x in far], owners, targets, rows))


def solution(mesh):
    in_specs = (
        P("section", None, None),
        P("section", None, None),
        P("section", None, None),
        P(),
        P(),
        P("section", None, None),
    )
    out_specs = (
        P(("dp", "section"), None, None, None),
        P(("dp", "section"), None, None, None),
        P(("dp", "section"), None, None),
    )
    return jax.shard_map(local, mesh=mesh, in_specs=in_specs, out_specs=out_specs, check_vma=False)
```

```python
import functools

import jax
import jax.numpy as jnp
from jax import lax
from jax.experimental import pallas as pl
from jax.experimental.pallas import tpu as pltpu
from jax.sharding import PartitionSpec as P


AXES = ("section", "dp")
BF16 = jnp.bfloat16
F32 = jnp.float32
CORE, Y_NEAR, Y_FAR, Z = 1, 2, 6, 8


def next_slot(count):
    order = list(range(0, count, 2)) + list(range(count - 1, 0, -2))
    return dict(zip(order[:-1], order[1:]))


def times(left, weights):
    return jnp.dot(left, weights, preferred_element_type=F32)


def times_t(left, weights):
    return lax.dot_general(left, weights, (((1,), (1,)), ((), ())), preferred_element_type=F32)


def first_kernel(early_ref, a_ref, h_ref, g_ref, w_ref, out_ref, grad_ref, turned_ref):
    early = early_ref[0] == 1

    @pl.when(pl.program_id(0) == 0)
    def _():
        turned_ref[...] = w_ref[0].T

    @pl.when(early)
    def _():
        out_ref[0, 0] = a_ref[0]
        product = times(h_ref[0], turned_ref[...])
        grad_ref[0, 0] = (g_ref[0].astype(F32) + product).astype(BF16)

    @pl.when(jnp.logical_not(early))
    def _():
        product = times(a_ref[0], w_ref[0])
        out_ref[0, 0] = (product + h_ref[0].astype(F32)).astype(BF16)
        grad_ref[0, 0] = times(g_ref[0], turned_ref[...]).astype(BF16)


def first_tick(early, a, held, cot, weights):
    _, height, width = a.shape
    block = height // 4
    rows = pl.BlockSpec((1, block, width), lambda i: (0, i, 0))
    wide = pl.BlockSpec((1, 1, block, width), lambda i: (0, 0, i, 0))
    both = jax.ShapeDtypeStruct((1, 2, height, width), BF16)
    return pl.pallas_call(
        first_kernel,
        grid=(4,),
        in_specs=[
            pl.BlockSpec(memory_space=pltpu.SMEM),
            rows,
            rows,
            rows,
            pl.BlockSpec((1, width, width), lambda i: (0, 0, 0)),
        ],
        out_specs=[wide, wide],
        out_shape=[both, both],
        scratch_shapes=[pltpu.VMEM((width, width), BF16)],
        cost_estimate=pl.CostEstimate(
            flops=4 * height * width * width, bytes_accessed=14 * height * width, transcendentals=0
        ),
        compiler_params=pltpu.CompilerParams(vmem_limit_bytes=60 << 20),
        name="first_tick",
    )(jnp.reshape(early.astype(jnp.int32), (1,)), a, held, cot, weights)


def place_kernel(plan, rows, replica_ref, *refs):
    pieces, targets, sem = refs[: len(plan)], refs[-4:-1], refs[-1]
    replica = replica_ref[0]
    views = (targets[0].at[0, 1], targets[1].at[0, 1], targets[2].at[0])
    copies = []
    for piece, blocks in zip(pieces, plan):
        for k, (output, mask) in enumerate(blocks):
            at = pl.multiple_of((replica ^ mask) * rows, rows)
            copies.append(
                pltpu.make_async_copy(
                    piece.at[pl.ds(k * rows, rows)],
                    views[output].at[pl.ds(at, rows)],
                    sem.at[len(copies)],
                )
            )
    for copy in copies:
        copy.start()
    for copy in copies:
        copy.wait()


def place(replica, pieces, plan, targets, rows):
    anywhere = pl.BlockSpec(memory_space=pl.ANY)
    width = targets[0].shape[-1]
    arrived = jax.ShapeDtypeStruct((1,) + targets[0].shape[2:], BF16)
    blocks = sum(len(some) for some in plan)
    return pl.pallas_call(
        functools.partial(place_kernel, plan, rows),
        in_specs=[pl.BlockSpec(memory_space=pltpu.SMEM)]
        + [pl.BlockSpec(memory_space=pltpu.VMEM)] * len(pieces)
        + [anywhere] * len(targets),
        out_specs=[anywhere] * 3,
        out_shape=[jax.ShapeDtypeStruct(x.shape, BF16) for x in targets[:2]] + [arrived],
        scratch_shapes=[pltpu.SemaphoreType.DMA((blocks,))],
        input_output_aliases={1 + len(pieces) + k: k for k in range(len(targets))},
        compiler_params=pltpu.CompilerParams(vmem_limit_bytes=8 << 20),
        cost_estimate=pl.CostEstimate(
            flops=0, bytes_accessed=4 * blocks * rows * width, transcendentals=0
        ),
    )(replica, *pieces, *targets)


def local(
    section_inputs, mirror_held, section_cotangents, next_batch, loss_cotangent, join_weights
):
    count = lax.axis_size("section")
    replicas = lax.axis_size("dp")
    position = lax.axis_index("section")
    replica = lax.axis_index("dp")
    is_early = position % 2 == 0
    weights = join_weights[0]
    rows = next_batch.shape[0] // replicas
    end = count - 1
    tie = lax.optimization_barrier

    def send(value, *moves):
        chosen = []
        for slots, flip in moves:
            for s, t in slots:
                chosen += [(s * replicas + d, t * replicas + (d ^ flip)) for d in range(replicas)]
        return lax.ppermute(value, AXES, chosen)

    after = next_slot(count)
    early = range(0, count, 2)
    late = range(1, count, 2)
    ahead = list(after.items())
    back = [(t, s) for s, t in ahead] + [(0, 1)]
    ahead += [(1, 0)]
    to_late = [(s, s + 1) for s in early]
    to_early = [(s, s - 1) for s in late]
    across = [(s, (s + 1) % count) for s in late]

    def part(whole, of):
        return lax.dynamic_slice_in_dim(whole, of * rows, rows, 0)

    sent = replica ^ Z
    a, held, cot = section_inputs[0], mirror_held[0], section_cotangents[0]
    a_part, held_part, cot_part = part(a, sent), part(held, sent), part(cot, sent)
    loss_part, batch_part = part(loss_cotangent, sent), part(next_batch, sent)
    product = times(a_part, weights)
    skip = product.astype(BF16)
    late_out = (product + held_part.astype(F32)).astype(BF16)
    out = jnp.where(is_early, a_part, jnp.where(position == 1, batch_part, late_out))
    level = jnp.where(is_early, skip, cot_part)
    came_out = send(out, (ahead, Z))
    came_level = send(level, (to_late, Z), (to_early, Z))
    product = times_t(jnp.where(is_early, held_part, cot_part), weights)
    grad = jnp.where(is_early, cot_part.astype(F32) + product, product).astype(BF16)
    grad_back = jnp.where(position == 0, loss_part, grad)
    grad_across = jnp.where(position == end, loss_part, grad)
    grad_back, grad_across = tie((grad_back, grad_across))
    came_grad = send(grad_back, (back, Z))

    product = times(came_out, weights)
    sent_on = jnp.where(is_early, product.astype(BF16), grad_across)
    arrived = send(sent_on, (to_late, 0), (across, Z))
    late_out = (product + came_level.astype(F32)).astype(BF16)
    second_out = jnp.where(is_early, came_out, late_out)
    product = times_t(jnp.where(is_early, came_level, came_grad), weights)
    second_grad = jnp.where(is_early, came_grad.astype(F32) + product, product).astype(BF16)

    everyone = [(s, s) for s in range(count)]

    def hop(value, mask):
        return send(value, (everyone, mask))

    orders = ((Y_NEAR, Y_FAR, Z), (Y_FAR, Z, Y_NEAR), (Z, Y_NEAR, Y_FAR))
    held_rows = [second_out, second_grad, arrived]
    masks = [[0], [0], [0]]
    for step in range(2):
        came = [hop(x, orders[k][step]) for k, x in enumerate(held_rows)]
        held_rows = [jnp.concatenate([x, y], axis=0) for x, y in zip(held_rows, came)]
        masks = [m + [k ^ order[step] for k in m] for m, order in zip(masks, orders)]
    last = [hop(x, orders[k][2]) for k, x in enumerate(held_rows)]
    plan = [[(k, m) for m in some] for k, some in enumerate(masks)]
    last_plan = [[(k, m ^ orders[k][2]) for k, m in blocks] for blocks in plan]
    partner = lambda plans: [[(k, m ^ CORE) for k, m in blocks] for blocks in plans]

    outs, grads = first_tick(
        is_early, section_inputs, mirror_held, section_cotangents, join_weights
    )
    near = [hop(x, CORE) for x in held_rows]
    here = jnp.reshape(replica, (1,))
    targets = place(here, held_rows + near, plan + partner(plan), (outs, grads), rows)
    last, targets = tie((last, targets))
    far = [hop(x, CORE) for x in last]
    targets = place(here, last, last_plan, targets, rows)
    return tuple(place(here, far, partner(last_plan), targets, rows))


def solution(mesh):
    in_specs = (
        P("section", None, None),
        P("section", None, None),
        P("section", None, None),
        P(),
        P(),
        P("section", None, None),
    )
    out_specs = (
        P(("dp", "section"), None, None, None),
        P(("dp", "section"), None, None, None),
        P(("dp", "section"), None, None),
    )
    return jax.shard_map(local, mesh=mesh, in_specs=in_specs, out_specs=out_specs, check_vma=False)
```

```python
import functools

import jax
import jax.numpy as jnp
from jax import lax
from jax.experimental import pallas as pl
from jax.experimental.pallas import tpu as pltpu
from jax.sharding import PartitionSpec as P


AXES = ("section", "dp")
BF16 = jnp.bfloat16
F32 = jnp.float32
CORE, Y_NEAR, Y_FAR, Z = 1, 2, 6, 8


def next_slot(count):
    order = list(range(0, count, 2)) + list(range(count - 1, 0, -2))
    return dict(zip(order[:-1], order[1:]))


def times(left, weights):
    return jnp.dot(left, weights, preferred_element_type=F32)


def times_t(left, weights):
    return lax.dot_general(left, weights, (((1,), (1,)), ((), ())), preferred_element_type=F32)


def first_kernel(
    spec_ref, a_ref, h_ref, g_ref, w_ref, out_ref, grad_ref, mine_ref, a_in, h_in, g_in, w_in, out_buf, grad_buf, in_sem, out_sem
):
    early = spec_ref[0] == 1
    height, width = a_in.shape
    start = pl.multiple_of(spec_ref[1] * height, height)
    part = width // 4
    rows = pl.ds(start, height)
    come = [
        pltpu.make_async_copy(ref.at[0, rows], buf, in_sem.at[n])
        for n, (ref, buf) in enumerate(((h_ref, h_in), (g_ref, g_in), (a_ref, a_in)))
    ]
    turn = [
        pltpu.make_async_copy(
            w_ref.at[0, pl.ds(k * part, part)], w_in.at[pl.ds(k * part, part)], in_sem.at[3 + k]
        )
        for k in range(4)
    ]

    def go(buf, ref, n):
        return [
            pltpu.make_async_copy(buf, ref.at[0, 0, rows], out_sem.at[n]),
            pltpu.make_async_copy(buf, mine_ref.at[n], out_sem.at[2 + n]),
        ]

    for copy in turn[:2] + come + turn[2:]:
        copy.start()
    for copy in turn + come:
        copy.wait()

    @pl.when(early)
    def _():
        for copy in go(a_in, out_ref, 0):
            copy.start()
        product = times_t(h_in[...], w_in[...])
        grad_buf[...] = (g_in[...].astype(F32) + product).astype(BF16)

    @pl.when(jnp.logical_not(early))
    def _():
        product = times(a_in[...], w_in[...])
        out_buf[...] = (product + h_in[...].astype(F32)).astype(BF16)
        for copy in go(out_buf, out_ref, 0):
            copy.start()
        grad_buf[...] = times_t(g_in[...], w_in[...]).astype(BF16)

    for copy in go(grad_buf, grad_ref, 1):
        copy.start()
    for copy in go(out_buf, out_ref, 0) + go(grad_buf, grad_ref, 1):
        copy.wait()


def first_tick(early, core, a, held, cot, weights):
    _, height, width = a.shape
    half = height // 2
    anywhere = pl.BlockSpec(memory_space=pl.ANY)
    both = jax.ShapeDtypeStruct((1, 2, height, width), BF16)
    return pl.pallas_call(
        first_kernel,
        in_specs=[pl.BlockSpec(memory_space=pltpu.SMEM)] + [anywhere] * 4,
        out_specs=[anywhere] * 3,
        out_shape=[both, both, jax.ShapeDtypeStruct((2, half, width), BF16)],
        scratch_shapes=[pltpu.VMEM((half, width), BF16)] * 3
        + [pltpu.VMEM((width, width), BF16)]
        + [pltpu.VMEM((half, width), BF16)] * 2
        + [pltpu.SemaphoreType.DMA((7,)), pltpu.SemaphoreType.DMA((4,))],
        cost_estimate=pl.CostEstimate(
            flops=2 * height * width * width, bytes_accessed=8 * height * width, transcendentals=0
        ),
        compiler_params=pltpu.CompilerParams(vmem_limit_bytes=60 << 20),
        name="first_tick",
    )(jnp.stack([early.astype(jnp.int32), core]), a, held, cot, weights)


def place_kernel(plan, rows, halves, replica_ref, *refs):
    pieces, targets, sem = refs[: len(plan)], refs[-4:-1], refs[-1]
    other = refs[len(plan)] if halves else None
    replica = replica_ref[0]
    views = (targets[0].at[0, 1], targets[1].at[0, 1], targets[2].at[0])
    copies = []
    for piece, blocks in zip(pieces, plan):
        for k, (output, mask) in enumerate(blocks):
            at = pl.multiple_of((replica ^ mask) * rows, rows)
            copies.append(
                pltpu.make_async_copy(
                    piece.at[pl.ds(k * rows, rows)],
                    views[output].at[pl.ds(at, rows)],
                    sem.at[len(copies)],
                )
            )
    if halves:
        half = other.shape[1]
        at = pl.ds(pl.multiple_of((1 - replica % 2) * half, half), half)
        for k in range(2):
            view = targets[k].at[0, 0, at]
            copies.append(pltpu.make_async_copy(other.at[k], view, sem.at[len(copies)]))
    for copy in copies:
        copy.start()
    for copy in copies:
        copy.wait()


def place(replica, pieces, plan, targets, rows, halves=()):
    anywhere = pl.BlockSpec(memory_space=pl.ANY)
    width = targets[0].shape[-1]
    arrived = jax.ShapeDtypeStruct((1,) + targets[0].shape[2:], BF16)
    blocks = sum(len(some) for some in plan)
    return pl.pallas_call(
        functools.partial(place_kernel, plan, rows, len(halves) > 0),
        in_specs=[pl.BlockSpec(memory_space=pltpu.SMEM)]
        + [pl.BlockSpec(memory_space=pltpu.VMEM)] * (len(pieces) + len(halves))
        + [anywhere] * len(targets),
        out_specs=[anywhere] * 3,
        out_shape=[jax.ShapeDtypeStruct(x.shape, BF16) for x in targets[:2]] + [arrived],
        scratch_shapes=[pltpu.SemaphoreType.DMA((blocks + 2 * len(halves),))],
        input_output_aliases={
            1 + len(pieces) + len(halves) + k: k for k in range(len(targets))
        },
        compiler_params=pltpu.CompilerParams(vmem_limit_bytes=8 << 20),
        cost_estimate=pl.CostEstimate(
            flops=0, bytes_accessed=4 * blocks * rows * width, transcendentals=0
        ),
    )(replica, *pieces, *halves, *targets)


def local(
    section_inputs, mirror_held, section_cotangents, next_batch, loss_cotangent, join_weights
):
    count = lax.axis_size("section")
    replicas = lax.axis_size("dp")
    position = lax.axis_index("section")
    replica = lax.axis_index("dp")
    is_early = position % 2 == 0
    weights = join_weights[0]
    rows = next_batch.shape[0] // replicas
    end = count - 1
    tie = lax.optimization_barrier

    def send(value, *moves):
        chosen = []
        for slots, flip in moves:
            for s, t in slots:
                chosen += [(s * replicas + d, t * replicas + (d ^ flip)) for d in range(replicas)]
        return lax.ppermute(value, AXES, chosen)

    after = next_slot(count)
    early = range(0, count, 2)
    late = range(1, count, 2)
    ahead = list(after.items())
    back = [(t, s) for s, t in ahead] + [(0, 1)]
    ahead += [(1, 0)]
    to_late = [(s, s + 1) for s in early]
    to_early = [(s, s - 1) for s in late]
    across = [(s, (s + 1) % count) for s in late]

    def part(whole, of):
        return lax.dynamic_slice_in_dim(whole, of * rows, rows, 0)

    sent = replica ^ Z
    a, held, cot = section_inputs[0], mirror_held[0], section_cotangents[0]
    a_part, held_part, cot_part = part(a, sent), part(held, sent), part(cot, sent)
    loss_part, batch_part = part(loss_cotangent, sent), part(next_batch, sent)
    product = times(a_part, weights)
    skip = product.astype(BF16)
    late_out = (product + held_part.astype(F32)).astype(BF16)
    out = jnp.where(is_early, a_part, jnp.where(position == 1, batch_part, late_out))
    level = jnp.where(is_early, skip, cot_part)
    came_out = send(out, (ahead, Z))
    came_level = send(level, (to_late, Z), (to_early, Z))
    product = times_t(jnp.where(is_early, held_part, cot_part), weights)
    grad = jnp.where(is_early, cot_part.astype(F32) + product, product).astype(BF16)
    grad_back = jnp.where(position == 0, loss_part, grad)
    grad_across = jnp.where(position == end, loss_part, grad)
    grad_back, grad_across = tie((grad_back, grad_across))
    came_grad = send(grad_back, (back, Z))

    product = times(came_out, weights)
    sent_on = jnp.where(is_early, product.astype(BF16), grad_across)
    arrived = send(sent_on, (to_late, 0), (across, Z))
    came_out = tie(came_out)
    late_out = (times(came_out, weights) + came_level.astype(F32)).astype(BF16)
    second_out = jnp.where(is_early, came_out, late_out)
    product = times_t(jnp.where(is_early, came_level, came_grad), weights)
    second_grad = jnp.where(is_early, came_grad.astype(F32) + product, product).astype(BF16)

    everyone = [(s, s) for s in range(count)]

    def hop(value, mask):
        return send(value, (everyone, mask))

    orders = ((Y_NEAR, Y_FAR, Z), (Y_FAR, Z, Y_NEAR), (Z, Y_NEAR, Y_FAR))
    held_rows = [second_out, second_grad, arrived]
    masks = [[0], [0], [0]]
    for step in range(2):
        came = [hop(x, orders[k][step]) for k, x in enumerate(held_rows)]
        held_rows = [jnp.concatenate([x, y], axis=0) for x, y in zip(held_rows, came)]
        masks = [m + [k ^ order[step] for k in m] for m, order in zip(masks, orders)]
    last = [hop(x, orders[k][2]) for k, x in enumerate(held_rows)]
    plan = [[(k, m) for m in some] for k, some in enumerate(masks)]
    last_plan = [[(k, m ^ orders[k][2]) for k, m in blocks] for blocks in plan]
    partner = lambda plans: [[(k, m ^ CORE) for k, m in blocks] for blocks in plans]

    outs, grads, mine = first_tick(
        is_early, replica % 2, section_inputs, mirror_held, section_cotangents, join_weights
    )
    other = hop(mine, CORE)
    near = [hop(x, CORE) for x in held_rows]
    here = jnp.reshape(replica, (1,))
    targets = place(here, held_rows + near, plan + partner(plan), (outs, grads), rows)
    targets = place(here, [], [], targets, rows, (other,))
    far = [hop(x, CORE) for x in last]
    far_plan = partner(last_plan)
    targets = place(here, last + far[:2], last_plan + far_plan[:2], targets, rows)
    return tuple(place(here, far[2:], far_plan[2:], targets, rows))


def solution(mesh):
    in_specs = (
        P("section", None, None),
        P("section", None, None),
        P("section", None, None),
        P(),
        P(),
        P("section", None, None),
    )
    out_specs = (
        P(("dp", "section"), None, None, None),
        P(("dp", "section"), None, None, None),
        P(("dp", "section"), None, None),
    )
    return jax.shard_map(local, mesh=mesh, in_specs=in_specs, out_specs=out_specs, check_vma=False)
```

```python
import functools

import jax
import jax.numpy as jnp
from jax import lax
from jax.experimental import pallas as pl
from jax.experimental.pallas import tpu as pltpu
from jax.sharding import PartitionSpec as P


AXES = ("section", "dp")
BF16 = jnp.bfloat16
F32 = jnp.float32
CORE, Y_NEAR, Y_FAR, Z = 1, 2, 6, 8


def next_slot(count):
    order = list(range(0, count, 2)) + list(range(count - 1, 0, -2))
    return dict(zip(order[:-1], order[1:]))


def times(left, weights):
    return jnp.dot(left, weights, preferred_element_type=F32)


def times_t(left, weights):
    return lax.dot_general(left, weights, (((1,), (1,)), ((), ())), preferred_element_type=F32)


def first_kernel(
    early_ref, core_ref, a_ref, h_ref, g_ref, w_ref, out_ref, grad_ref, mine_ref, a_in, h_in, g_in, w_in, out_buf, grad_buf, in_sem, out_sem
):
    early = early_ref[0] == 1
    height, width = a_in.shape
    start = pl.multiple_of(core_ref[0] * height, height)
    part = width // 4
    rows = pl.ds(start, height)
    come = [
        pltpu.make_async_copy(ref.at[0, rows], buf, in_sem.at[n])
        for n, (ref, buf) in enumerate(((h_ref, h_in), (g_ref, g_in), (a_ref, a_in)))
    ]
    turn = [
        pltpu.make_async_copy(
            w_ref.at[0, pl.ds(k * part, part)], w_in.at[pl.ds(k * part, part)], in_sem.at[3 + k]
        )
        for k in range(4)
    ]

    def go(buf, ref, n):
        return [
            pltpu.make_async_copy(buf, ref.at[0, 0, rows], out_sem.at[n]),
            pltpu.make_async_copy(buf, mine_ref.at[n], out_sem.at[2 + n]),
        ]

    take_h, take_g, take_a = come
    for copy in [take_a, take_g] + turn + [take_h]:
        copy.start()

    @pl.when(early)
    def _():
        take_a.wait()
        for copy in go(a_in, out_ref, 0):
            copy.start()
        for copy in turn + [take_h, take_g]:
            copy.wait()
        product = times_t(h_in[...], w_in[...])
        grad_buf[...] = (g_in[...].astype(F32) + product).astype(BF16)

    @pl.when(jnp.logical_not(early))
    def _():
        for copy in turn + [take_a, take_h]:
            copy.wait()
        product = times(a_in[...], w_in[...])
        out_buf[...] = (product + h_in[...].astype(F32)).astype(BF16)
        for copy in go(out_buf, out_ref, 0):
            copy.start()
        take_g.wait()
        grad_buf[...] = times_t(g_in[...], w_in[...]).astype(BF16)

    for copy in go(grad_buf, grad_ref, 1):
        copy.start()
    for copy in go(out_buf, out_ref, 0) + go(grad_buf, grad_ref, 1):
        copy.wait()


def first_tick(early, core, a, held, cot, weights):
    _, height, width = a.shape
    half = height // 2
    anywhere = pl.BlockSpec(memory_space=pl.ANY)
    both = jax.ShapeDtypeStruct((1, 2, height, width), BF16)
    call = pl.pallas_call(
        first_kernel,
        in_specs=[pl.BlockSpec(memory_space=pltpu.SMEM)] * 2 + [anywhere] * 4,
        out_specs=[anywhere] * 3,
        out_shape=[both, both, jax.ShapeDtypeStruct((2, half, width), BF16)],
        scratch_shapes=[pltpu.VMEM((half, width), BF16)] * 3
        + [pltpu.VMEM((width, width), BF16)]
        + [pltpu.VMEM((half, width), BF16)] * 2
        + [pltpu.SemaphoreType.DMA((7,)), pltpu.SemaphoreType.DMA((4,))],
        cost_estimate=pl.CostEstimate(
            flops=2 * height * width * width, bytes_accessed=8 * height * width, transcendentals=0
        ),
        compiler_params=pltpu.CompilerParams(vmem_limit_bytes=60 << 20),
        name="first_tick",
    )
    scalars = (jnp.reshape(x.astype(jnp.int32), (1,)) for x in (early, core))
    return call(*scalars, a, held, cot, weights)


def place_kernel(plan, rows, halves, replica_ref, *refs):
    pieces, targets, sem = refs[: len(plan)], refs[-4:-1], refs[-1]
    other = refs[len(plan)] if halves else None
    replica = replica_ref[0]
    views = (targets[0].at[0, 1], targets[1].at[0, 1], targets[2].at[0])
    copies = []
    for piece, blocks in zip(pieces, plan):
        for k, (output, mask) in enumerate(blocks):
            at = pl.multiple_of((replica ^ mask) * rows, rows)
            copies.append(
                pltpu.make_async_copy(
                    piece.at[pl.ds(k * rows, rows)],
                    views[output].at[pl.ds(at, rows)],
                    sem.at[len(copies)],
                )
            )
    if halves:
        half = other.shape[1]
        at = pl.ds(pl.multiple_of((1 - replica % 2) * half, half), half)
        for k in range(2):
            view = targets[k].at[0, 0, at]
            copies.append(pltpu.make_async_copy(other.at[k], view, sem.at[len(copies)]))
    for copy in copies:
        copy.start()
    for copy in copies:
        copy.wait()


def place(replica, pieces, plan, targets, rows, halves=()):
    anywhere = pl.BlockSpec(memory_space=pl.ANY)
    width = targets[0].shape[-1]
    arrived = jax.ShapeDtypeStruct((1,) + targets[0].shape[2:], BF16)
    blocks = sum(len(some) for some in plan)
    return pl.pallas_call(
        functools.partial(place_kernel, plan, rows, len(halves) > 0),
        in_specs=[pl.BlockSpec(memory_space=pltpu.SMEM)]
        + [pl.BlockSpec(memory_space=pltpu.VMEM)] * (len(pieces) + len(halves))
        + [anywhere] * len(targets),
        out_specs=[anywhere] * 3,
        out_shape=[jax.ShapeDtypeStruct(x.shape, BF16) for x in targets[:2]] + [arrived],
        scratch_shapes=[pltpu.SemaphoreType.DMA((blocks + 2 * len(halves),))],
        input_output_aliases={
            1 + len(pieces) + len(halves) + k: k for k in range(len(targets))
        },
        compiler_params=pltpu.CompilerParams(vmem_limit_bytes=8 << 20),
        cost_estimate=pl.CostEstimate(
            flops=0, bytes_accessed=4 * blocks * rows * width, transcendentals=0
        ),
    )(replica, *pieces, *halves, *targets)


def local(
    section_inputs, mirror_held, section_cotangents, next_batch, loss_cotangent, join_weights
):
    count = lax.axis_size("section")
    replicas = lax.axis_size("dp")
    position = lax.axis_index("section")
    replica = lax.axis_index("dp")
    is_early = position % 2 == 0
    weights = join_weights[0]
    rows = next_batch.shape[0] // replicas
    end = count - 1
    tie = lax.optimization_barrier

    def send(value, *moves):
        chosen = []
        for slots, flip in moves:
            for s, t in slots:
                chosen += [(s * replicas + d, t * replicas + (d ^ flip)) for d in range(replicas)]
        return lax.ppermute(value, AXES, chosen)

    after = next_slot(count)
    early = range(0, count, 2)
    late = range(1, count, 2)
    ahead = list(after.items())
    back = [(t, s) for s, t in ahead] + [(0, 1)]
    ahead += [(1, 0)]
    to_late = [(s, s + 1) for s in early]
    to_early = [(s, s - 1) for s in late]
    across = [(s, (s + 1) % count) for s in late]

    def part(whole, of):
        return lax.dynamic_slice_in_dim(whole, of * rows, rows, 0)

    sent = replica ^ Z
    a, held, cot = section_inputs[0], mirror_held[0], section_cotangents[0]
    a_part, held_part, cot_part = part(a, sent), part(held, sent), part(cot, sent)
    loss_part, batch_part = part(loss_cotangent, sent), part(next_batch, sent)
    product = times(a_part, weights)
    skip = product.astype(BF16)
    late_out = (product + held_part.astype(F32)).astype(BF16)
    out = jnp.where(is_early, a_part, jnp.where(position == 1, batch_part, late_out))
    level = jnp.where(is_early, skip, cot_part)
    came_out = send(out, (ahead, Z))
    came_level = send(level, (to_late, Z), (to_early, Z))
    product = times_t(jnp.where(is_early, held_part, cot_part), weights)
    grad = jnp.where(is_early, cot_part.astype(F32) + product, product).astype(BF16)
    grad_back = jnp.where(position == 0, loss_part, grad)
    grad_across = jnp.where(position == end, loss_part, grad)
    grad_back, grad_across = tie((grad_back, grad_across))
    came_grad = send(grad_back, (back, Z))

    product = times(came_out, weights)
    sent_on = jnp.where(is_early, product.astype(BF16), grad_across)
    arrived = send(sent_on, (to_late, 0), (across, Z))
    came_out = tie(came_out)
    late_out = (times(came_out, weights) + came_level.astype(F32)).astype(BF16)
    second_out = jnp.where(is_early, came_out, late_out)
    product = times_t(jnp.where(is_early, came_level, came_grad), weights)
    second_grad = jnp.where(is_early, came_grad.astype(F32) + product, product).astype(BF16)

    everyone = [(s, s) for s in range(count)]

    def hop(value, mask):
        return send(value, (everyone, mask))

    orders = ((Y_NEAR, Y_FAR, Z), (Y_FAR, Z, Y_NEAR), (Z, Y_NEAR, Y_FAR))
    held_rows = [second_out, second_grad, arrived]
    masks = [[0], [0], [0]]
    for step in range(2):
        came = [hop(x, orders[k][step]) for k, x in enumerate(held_rows)]
        held_rows = [jnp.concatenate([x, y], axis=0) for x, y in zip(held_rows, came)]
        masks = [m + [k ^ order[step] for k in m] for m, order in zip(masks, orders)]
    last = [hop(x, orders[k][2]) for k, x in enumerate(held_rows)]
    plan = [[(k, m) for m in some] for k, some in enumerate(masks)]
    last_plan = [[(k, m ^ orders[k][2]) for k, m in blocks] for blocks in plan]
    partner = lambda plans: [[(k, m ^ CORE) for k, m in blocks] for blocks in plans]

    outs, grads, mine = first_tick(
        is_early, replica % 2, section_inputs, mirror_held, section_cotangents, join_weights
    )
    other = hop(mine, CORE)
    near = [hop(x, CORE) for x in held_rows]
    here = jnp.reshape(replica, (1,))
    targets = place(here, held_rows + near, plan + partner(plan), (outs, grads), rows)
    targets = place(here, [], [], targets, rows, (other,))
    far = [hop(x, CORE) for x in last]
    far_plan = partner(last_plan)
    targets = place(here, last + far[:2], last_plan + far_plan[:2], targets, rows)
    return tuple(place(here, far[2:], far_plan[2:], targets, rows))


def solution(mesh):
    in_specs = (
        P("section", None, None),
        P("section", None, None),
        P("section", None, None),
        P(),
        P(),
        P("section", None, None),
    )
    out_specs = (
        P(("dp", "section"), None, None, None),
        P(("dp", "section"), None, None, None),
        P(("dp", "section"), None, None),
    )
    return jax.shard_map(local, mesh=mesh, in_specs=in_specs, out_specs=out_specs, check_vma=False)
```
